32 devices in a mesh: layer: 16 (over z, x, core), tile: 2 (over y).
Axes of the slice: x: 2, y: 2, z: 4, core: 2. Of those that a mesh axis runs over, the one named last changes fastest.
Arguments:
- sources: bfloat16 [16, 2, 160, 1024], P('layer', None, None, 'tile'), may hold values from -6 to 6
- near_block: bfloat16 [16, 2, 2, 512, 512], P('layer', 'tile'), may hold values from -0.1875 to 0.1875
- expand_basis: bfloat16 [16, 2, 2, 2, 96, 512], P('layer', 'tile'), may hold values from -0.4375 to 0.4375
- compress_basis: bfloat16 [16, 2, 2, 2, 96, 512], P('layer', 'tile'), may hold values from -0.1875 to 0.1875
- mode_basis: bfloat16 [16, 2, 2, 512, 128], P('layer', 'tile'), may hold values from -0.1875 to 0.1875
- down_factor: float32 [16, 2, 2, 128], P('layer', 'tile'), may hold values from -1 to 1, as said below
- up_factor: float32 [16, 2, 2, 128], P('layer', 'tile'), may hold values from -1 to 1, as said below
- far_ranks: int32 [16, 2, 2], P('layer'), may hold values from 16 to 96, as said below
Outputs:
- layer_field: bfloat16 [16, 2, 160, 1024], P('layer', None, None, 'tile')
The draws below stay inside these ranges and needn't reach their ends.
Inputs may be any that keep to these rules, and one draw needn't show every extreme that they name: `down_factor`: every complex factor has modulus at most 1. `up_factor`: every complex factor has modulus at most 1. `far_ranks`: entries with target equal to source are unused; some off-diagonal entry equals 96 and some equals 16.
All inputs are finite; a program needn't handle non-finite values.
Results may differ from the reference program's by a relative error of at most 0.0085.
Values may be sent and summed in bfloat16 or wider, within the bound.
A program may use at most 64 MiB of HBM per device.

```python
import math
import jax
import jax.numpy as jnp
from jax import lax

TRACE = 512
HARMONIC_TOTAL = 128
RMAX = 96
RLO = 16
SRC = 160
PATCH_TOTAL = 2
WIDTH = 1024
SLAB_TOTAL = 16


def factor_law(key, salt):
    copy_channels = jax.random.split(jax.random.fold_in(key, salt), 8)
    slow_share = 0.5
    slow_pick = jax.random.uniform(copy_channels[0], (PATCH_TOTAL, HARMONIC_TOTAL)) < slow_share
    slow_rate = jnp.exp(jax.random.uniform(copy_channels[1], (PATCH_TOTAL, HARMONIC_TOTAL), jnp.float32, math.log(0.1), math.log(0.4))) / SLAB_TOTAL
    fast_rate = jnp.exp(jax.random.uniform(copy_channels[2], (PATCH_TOTAL, HARMONIC_TOTAL), jnp.float32, math.log(1.0 / 16.0), math.log(0.25)))
    base_rate = jnp.where(slow_pick, slow_rate, fast_rate)
    device_scale = jnp.exp(jax.random.uniform(copy_channels[3], (SLAB_TOTAL, PATCH_TOTAL, 1), jnp.float32, math.log(0.5), math.log(2.0)))
    copy_speeds = base_rate[None] * device_scale
    slab_index = jnp.arange(SLAB_TOTAL).astype(jnp.int32)[:, None, None]
    first_packet = jax.random.randint(copy_channels[4], (PATCH_TOTAL, HARMONIC_TOTAL), 0, SLAB_TOTAL)
    final_packet = jax.random.randint(copy_channels[5], (PATCH_TOTAL, HARMONIC_TOTAL), 0, SLAB_TOTAL)
    packet_extents = jax.random.uniform(copy_channels[6], (2, PATCH_TOTAL, HARMONIC_TOTAL), jnp.float32, 0.5, 0.8)
    packet_extent = jnp.where(slab_index == first_packet[None], packet_extents[0][None], 1.0)
    packet_extent = packet_extent * jnp.where(slab_index == final_packet[None], packet_extents[1][None], 1.0)
    quotient_base = jnp.exp(-copy_speeds) * packet_extent
    phase = jax.random.uniform(copy_channels[7], (SLAB_TOTAL, PATCH_TOTAL, HARMONIC_TOTAL), jnp.float32, -math.pi, math.pi)
    return jnp.stack([quotient_base * jnp.cos(phase), quotient_base * jnp.sin(phase)], axis=2).astype(jnp.float32)


def draw_down_factor(key, part):
    return factor_law(key, 11)


def draw_up_factor(key, part):
    return factor_law(key, 23)


def draw_far_ranks(key, part):
    copy_channels = jax.random.split(jax.random.fold_in(key, 37), 6)
    ranks = jax.random.randint(copy_channels[0], (SLAB_TOTAL, PATCH_TOTAL, PATCH_TOTAL), RLO, RMAX + 1).astype(jnp.int32)
    flat = ranks.reshape(-1)
    layer_one = jax.random.randint(copy_channels[1], (), 0, SLAB_TOTAL)
    target_one = jax.random.randint(copy_channels[2], (), 0, PATCH_TOTAL)
    offset_one = jax.random.randint(copy_channels[3], (), 1, PATCH_TOTAL)
    layer_two = (layer_one + 1) % SLAB_TOTAL
    target_two = jax.random.randint(copy_channels[4], (), 0, PATCH_TOTAL)
    offset_two = jax.random.randint(copy_channels[5], (), 1, PATCH_TOTAL)
    place_one = (layer_one * PATCH_TOTAL + target_one) * PATCH_TOTAL + (target_one + offset_one) % PATCH_TOTAL
    place_two = (layer_two * PATCH_TOTAL + target_two) * PATCH_TOTAL + (target_two + offset_two) % PATCH_TOTAL
    flat = flat.at[place_one].set(RMAX)
    flat = flat.at[place_two].set(RLO)
    return flat.reshape(SLAB_TOTAL, PATCH_TOTAL, PATCH_TOTAL).astype(jnp.int32)


def steps_of(stream_key, shape, cuts, least, high):
    level = 1.0
    for position, blocks in cuts:
        draws = jax.random.uniform(jax.random.fold_in(jax.random.fold_in(stream_key, 6), position), (blocks,), jnp.float32, least / len(cuts), high / len(cuts))
        level = level * jnp.repeat(jnp.exp(draws), shape[position] // blocks).reshape((-1,) + (1,) * (len(shape) - 1 - position))
    return level


def scatter_about(key, dims, deviation, bound, cuts=(), kind=jnp.bfloat16):
    level = steps_of(key, dims, cuts, -0.22, 0.18) if cuts else 1.0
    values = jax.random.normal(key, dims, jnp.float32) * deviation * level
    return jnp.minimum(jnp.maximum(values, -bound), bound).astype(kind)


def setup_inputs(seed: int = 0) -> dict:
    keys = jax.random.split(jax.random.key(seed), 9)
    sources = scatter_about(keys[0], (SLAB_TOTAL, 2, SRC, WIDTH), 1.0, 6.0, ((0, 16), (3, 2)))
    near_block = scatter_about(keys[1], (SLAB_TOTAL, PATCH_TOTAL, 2, TRACE, TRACE), (2 * TRACE) ** -0.5, 0.1875, ((0, 16), (1, 2)))
    expand_basis = scatter_about(keys[2], (SLAB_TOTAL, PATCH_TOTAL, PATCH_TOTAL, 2, RMAX, TRACE), (2 * RMAX) ** -0.5, 0.4375, ((0, 16), (1, 2)))
    compress_basis = scatter_about(keys[3], (SLAB_TOTAL, PATCH_TOTAL, PATCH_TOTAL, 2, RMAX, TRACE), (2 * TRACE) ** -0.5, 0.1875, ((0, 16), (1, 2)))
    mode_basis = scatter_about(keys[4], (SLAB_TOTAL, PATCH_TOTAL, 2, TRACE, HARMONIC_TOTAL), (2 * TRACE) ** -0.5, 0.1875, ((0, 16), (1, 2)))
    down_factor = draw_down_factor(jax.random.fold_in(keys[8], 71), 0)
    up_factor = draw_up_factor(jax.random.fold_in(keys[8], 71), 0)
    far_ranks = draw_far_ranks(jax.random.fold_in(keys[8], 71), 0)
    return {"sources": sources, "near_block": near_block, "expand_basis": expand_basis, "compress_basis": compress_basis, "mode_basis": mode_basis, "down_factor": down_factor, "up_factor": up_factor, "far_ranks": far_ranks}


def complex_dot(a, b):
    real_part = jnp.dot(a[0], b[0], preferred_element_type=jnp.float32) - jnp.dot(a[1], b[1], preferred_element_type=jnp.float32)
    imag_part = jnp.dot(a[0], b[1], preferred_element_type=jnp.float32) + jnp.dot(a[1], b[0], preferred_element_type=jnp.float32)
    return jnp.stack([real_part, imag_part])


def complex_dot_back(a, b):
    return complex_dot(a, jnp.swapaxes(b, 1, 2))


def front_layer(entries):
    layer_sources, near_layer, expand_layer, compress_layer, mode_layer, rank_layer = entries
    tiled = layer_sources.reshape(2, SRC, PATCH_TOTAL, TRACE)
    rank_slots = jnp.arange(RMAX).astype(jnp.int32)

    def single_tile(target):
        own_traces = lax.dynamic_index_in_dim(tiled, target, 2, keepdims=False)
        near_part = complex_dot(own_traces, near_layer[target])

        def add_remote(running, source):
            remote = lax.dynamic_index_in_dim(tiled, source, 2, keepdims=False)
            coefficients = complex_dot_back(remote, compress_layer[target, source])
            kept_mask = (rank_slots < rank_layer[target, source]) & (source != target)
            coefficients = jnp.where(kept_mask, coefficients, jnp.float32(0.0)).astype(jnp.bfloat16)
            return running + complex_dot(coefficients, expand_layer[target, source]), None

        far_part, _ = lax.scan(add_remote, jnp.zeros((2, SRC, TRACE), jnp.float32), jnp.arange(PATCH_TOTAL).astype(jnp.int32))
        fronts = (near_part + far_part).astype(jnp.bfloat16)
        modal_part = complex_dot(fronts, mode_layer[target])
        return fronts, modal_part

    return lax.map(single_tile, jnp.arange(PATCH_TOTAL).astype(jnp.int32))


def sweep_step(carried, entries):
    factor, modal_part = entries
    factor_real = factor[:, 0][:, None, :]
    factor_imag = factor[:, 1][:, None, :]
    real_part = factor_real * carried[:, 0] - factor_imag * carried[:, 1] + modal_part[:, 0]
    imag_part = factor_real * carried[:, 1] + factor_imag * carried[:, 0] + modal_part[:, 1]
    return jnp.stack([real_part, imag_part], axis=1), carried


def back_layer(entries):
    fronts, incoming, mode_layer, near_layer = entries

    def single_tile(front_tile, in_tile, mode_tile, near_tile):
        back_part = complex_dot_back(in_tile, mode_tile).astype(jnp.bfloat16)
        return (front_tile.astype(jnp.float32) + complex_dot(back_part, near_tile)).astype(jnp.bfloat16)

    result = jax.vmap(single_tile)(fronts, incoming, mode_layer, near_layer)
    return jnp.transpose(result, (1, 2, 0, 3)).reshape(2, SRC, WIDTH)


def reference(sources, near_block, expand_basis, compress_basis, mode_basis, down_factor, up_factor, far_ranks):
    fronts, modal = lax.map(front_layer, (sources, near_block, expand_basis, compress_basis, mode_basis, far_ranks))
    start = jnp.zeros((PATCH_TOTAL, 2, SRC, HARMONIC_TOTAL), jnp.float32)
    _, down_in = lax.scan(sweep_step, start, (down_factor, modal))
    _, up_in = lax.scan(sweep_step, start, (up_factor, modal), reverse=True)
    incoming = (down_in + up_in).astype(jnp.bfloat16)
    return lax.map(back_layer, (fronts, incoming, mode_basis, near_block))
```

```python
import functools

import jax
import jax.numpy as jnp
from jax import lax
from jax.experimental import pallas as pl
from jax.experimental.pallas import tpu as pltpu
from jax.sharding import PartitionSpec as P

MESH = pl.DeviceIdType.MESH
F32 = jnp.float32
BF16 = jnp.bfloat16


def dot(a, b):
    return jnp.dot(a, b, preferred_element_type=F32)


def dot_back(a, b):
    return lax.dot_general(a, b, (((1,), (1,)), ((), ())), preferred_element_type=F32)


def complex_product(product, a, b_real, b_imag):
    a_real, a_imag = a
    return (
        product(a_real, b_real) - product(a_imag, b_imag),
        product(a_real, b_imag) + product(a_imag, b_real),
    )


def round_up(value, step):
    return (value + step - 1) // step * step


def group_size(layers):
    return 4 if layers % 4 == 0 else layers


def swap_place(place, group):
    return lax.rem(place, 2) * 2 + place // 2 if group == 4 else place


def complex_step(factor, value, addend):
    return (
        factor[0] * value[0] - factor[1] * value[1] + addend[0],
        factor[0] * value[1] + factor[1] * value[0] + addend[1],
    )


def kernel(
    layers, tiles, chunks, rows_each,
    ranks_hbm, src_hbm, near_hbm, expand_hbm, compress_hbm, mode_hbm, down_hbm, up_hbm,
    out,
    ranks, src, near, expand, compress, mode, factors, others,
    near_part, fronts, modal, outgoing, gathered, carries, entering, swept, returning, incoming,
    in_sem, src_send, src_recv, piece_send, piece_recv, carry_send, carry_recv,
    back_send, back_recv,
):
    layer = lax.axis_index("layer")
    tile = lax.axis_index("tile")
    count = src.shape[1]
    size = group_size(layers)
    groups = layers // size
    group = layer // size
    member = lax.rem(layer, size)
    place = swap_place(member, size)
    loads = [
        pltpu.make_async_copy(a, b, in_sem.at[i])
        for i, (a, b) in enumerate(
            [
                (src_hbm.at[0], src),
                (near_hbm.at[0, 0], near),
                (compress_hbm.at[0, 0], compress),
                (expand_hbm.at[0, 0], expand),
                (mode_hbm.at[0, 0], mode),
                (down_hbm.at[0, 0], factors.at[0]),
                (up_hbm.at[0, 0], factors.at[1]),
                (ranks_hbm.at[0], ranks),
            ]
        )
    ]
    for load in loads:
        load.start()

    barrier = pltpu.get_barrier_semaphore()
    for step in range(1, tiles):
        pl.semaphore_signal(
            barrier, inc=1, device_id=(layer, lax.rem(tile + step, tiles)), device_id_type=MESH
        )
    for step in range(1, size):
        peer = group * size + lax.rem(member + step, size)
        pl.semaphore_signal(barrier, inc=1, device_id=(peer, tile), device_id_type=MESH)
    for step in range(1, groups):
        peer = lax.rem(group + step, groups) * size + member
        pl.semaphore_signal(barrier, inc=1, device_id=(peer, tile), device_id_type=MESH)
    pl.semaphore_wait(barrier, tiles + size + groups - 3)

    loads[0].wait()
    exchanges = []
    for index, (first, length) in enumerate(chunks):
        part = []
        for step in range(1, tiles):
            copy = pltpu.make_async_remote_copy(
                src_ref=src.at[:, pl.ds(first, length)],
                dst_ref=others.at[step - 1, :, pl.ds(first, length)],
                send_sem=src_send.at[index, step - 1],
                recv_sem=src_recv.at[index, step - 1],
                device_id=(layer, lax.rem(tile + tiles - step, tiles)),
                device_id_type=MESH,
            )
            copy.start()
            part.append(copy)
        exchanges.append(part)

    loads[1].wait()
    real, imag = complex_product(dot, (src[0], src[1]), near[0], near[1])
    near_part[0] = real
    near_part[1] = imag
    for load in loads[2:]:
        load.wait()
    for p in range(size):
        for which in range(2):
            for half in range(2):
                at = 2 * rows_each + 2 * which + half
                outgoing[p, at : at + 1, :] = factors[which, half : half + 1, :]

    def piece_copy(p):
        target = (p % 2) * 2 + p // 2 if size == 4 else p
        return target, pltpu.make_async_remote_copy(
            src_ref=outgoing.at[p],
            dst_ref=gathered.at[member],
            send_sem=piece_send.at[p],
            recv_sem=piece_recv.at[member],
            device_id=(group * size + target, tile),
            device_id_type=MESH,
        )

    sent = 0
    for (first, length), part in zip(chunks, exchanges):
        rows = slice(first, first + length)
        far = [near_part[0, rows, :], near_part[1, rows, :]]
        for step in range(1, tiles):
            part[step - 1].wait_recv()
            source = lax.rem(tile + step, tiles)
            real, imag = complex_product(
                dot_back,
                (others[step - 1, 0, rows, :], others[step - 1, 1, rows, :]),
                compress[source, 0],
                compress[source, 1],
            )
            kept = lax.broadcasted_iota(jnp.int32, real.shape, 1) < ranks[tile, source]
            real = jnp.where(kept, real, 0.0).astype(BF16)
            imag = jnp.where(kept, imag, 0.0).astype(BF16)
            far_real, far_imag = complex_product(
                dot, (real, imag), expand[source, 0], expand[source, 1]
            )
            far = [far[0] + far_real, far[1] + far_imag]
        front = (far[0].astype(BF16), far[1].astype(BF16))
        fronts[0, rows, :] = front[0]
        fronts[1, rows, :] = front[1]
        real, imag = complex_product(dot, front, mode[0], mode[1])
        modal[0, rows, :] = real
        modal[1, rows, :] = imag
        places = []
        while sent < size and (
            (sent + 1) * rows_each <= first + length or first + length == count
        ):
            places.append(sent)
            sent += 1
        for p in places:
            own = slice(p * rows_each, (p + 1) * rows_each)
            outgoing[p, 0:rows_each, :] = modal[0, own, :]
            outgoing[p, rows_each : 2 * rows_each, :] = modal[1, own, :]
            target, copy = piece_copy(p)

            @pl.when(member != target)
            def _(copy=copy):
                copy.start()

    gathered[member] = outgoing[place]
    for sender in range(size):
        arrival = pltpu.make_async_remote_copy(
            src_ref=outgoing.at[0],
            dst_ref=gathered.at[sender],
            send_sem=piece_send.at[0],
            recv_sem=piece_recv.at[sender],
            device_id=(group * size + sender, tile),
            device_id_type=MESH,
        )

        @pl.when(member != sender)
        def _(arrival=arrival):
            arrival.wait_recv()

    reals, imags = slice(0, rows_each), slice(rows_each, 2 * rows_each)

    def pair(ref, at, row):
        return ref[at, row : row + 1, :], ref[at, row + 1 : row + 2, :]

    def factor_of(at, which):
        return pair(gathered, at, 2 * rows_each + 2 * which)

    def modal_of(at):
        return gathered[at, reals, :], gathered[at, imags, :]

    zero = jnp.zeros((rows_each, modal.shape[2]), F32)
    none = jnp.zeros((1, modal.shape[2]), F32)
    orders = [list(range(size)), list(range(size))[::-1]]
    for which, order in enumerate(orders):
        value = modal_of(order[0])
        product = factor_of(order[0], which)
        for at in order[1:]:
            factor = factor_of(at, which)
            value = complex_step(factor, value, modal_of(at))
            product = complex_step(factor, product, (none, none))
        carries[which, reals, :] = value[0]
        carries[which, imags, :] = value[1]
        carries[which, 2 * rows_each : 2 * rows_each + 1, :] = product[0]
        carries[which, 2 * rows_each + 1 : 2 * rows_each + 2, :] = product[1]

    def carry_copy(step, which):
        peer = (group + step if which == 0 else group - step) * size + member
        return pltpu.make_async_remote_copy(
            src_ref=carries.at[which],
            dst_ref=entering.at[group],
            send_sem=carry_send.at[which, step - 1],
            recv_sem=carry_recv.at[group],
            device_id=(peer, tile),
            device_id_type=MESH,
        )

    def each_carry(act):
        for step in range(groups - 1, 0, -1):

            @pl.when(group + step < groups)
            def _(step=step):
                act(carry_copy(step, 0))

            @pl.when(group - step >= 0)
            def _(step=step):
                act(carry_copy(step, 1))

    each_carry(lambda copy: copy.start())
    for other in range(groups):
        arrival = pltpu.make_async_remote_copy(
            src_ref=carries.at[0],
            dst_ref=entering.at[other],
            send_sem=carry_send.at[0, 0],
            recv_sem=carry_recv.at[other],
            device_id=(other * size + member, tile),
            device_id_type=MESH,
        )

        @pl.when(group != other)
        def _(arrival=arrival):
            arrival.wait_recv()

    def carried(others_order, before):
        value = (zero, zero)
        for other in others_order:
            after = complex_step(
                pair(entering, other, 2 * rows_each),
                value,
                (entering[other, reals, :], entering[other, imags, :]),
            )
            value = tuple(jnp.where(before(other), a, b) for a, b in zip(after, value))
        return value

    def back_copy(at):
        return pltpu.make_async_remote_copy(
            src_ref=returning.at[at],
            dst_ref=incoming.at[place],
            send_sem=back_send.at[at],
            recv_sem=back_recv.at[place],
            device_id=(group * size + at, tile),
            device_id_type=MESH,
        )

    value = carried(range(groups), lambda other: other < group)
    for at in range(size):
        swept[at, reals, :] = value[0]
        swept[at, imags, :] = value[1]
        if at < size - 1:
            value = complex_step(factor_of(at, 0), value, modal_of(at))
    value = carried(range(groups - 1, -1, -1), lambda other: other > group)
    for at in range(size - 1, -1, -1):
        whole = jnp.concatenate(
            [swept[at, reals, :] + value[0], swept[at, imags, :] + value[1]], axis=0
        )
        returning[at] = whole.reshape(returning.shape[1:]).astype(BF16)
        back = back_copy(at)

        @pl.when(member != at)
        def _(back=back):
            back.start()

        if at > 0:
            value = complex_step(factor_of(at, 1), value, modal_of(at))
    incoming[place] = returning[member]

    for p in range(size):
        target, _ = piece_copy(p)
        arrival = pltpu.make_async_remote_copy(
            src_ref=returning.at[0],
            dst_ref=incoming.at[p],
            send_sem=back_send.at[0],
            recv_sem=back_recv.at[p],
            device_id=(group * size + target, tile),
            device_id_type=MESH,
        )

        @pl.when(member != target)
        def _(arrival=arrival):
            arrival.wait_recv()

        piece = incoming[p].astype(F32).reshape(swept.shape[1:])
        own = slice(p * rows_each, (p + 1) * rows_each)
        modal[0, own, :] = piece[0:rows_each, :]
        modal[1, own, :] = piece[rows_each : 2 * rows_each, :]
    back = complex_product(
        dot_back, (modal[0, 0:count, :].astype(BF16), modal[1, 0:count, :].astype(BF16)),
        mode[0], mode[1],
    )
    real, imag = complex_product(
        dot, (back[0].astype(BF16), back[1].astype(BF16)), near[0], near[1]
    )
    out[0, 0] = (fronts[0].astype(F32) + real).astype(BF16)
    out[0, 1] = (fronts[1].astype(F32) + imag).astype(BF16)

    for part in exchanges:
        for copy in part:
            copy.wait_send()
    for p in range(size):
        target, copy = piece_copy(p)
        back = back_copy(p)

        @pl.when(member != target)
        def _(copy=copy):
            copy.wait_send()

        @pl.when(member != p)
        def _(back=back):
            back.wait_send()

    each_carry(lambda copy: copy.wait_send())


def solution(mesh):
    layers = mesh.shape["layer"]
    tiles = mesh.shape["tile"]

    def per_device(sources, near_block, expand_basis, compress_basis, mode_basis, down, up, ranks):
        _, _, count, traces = sources.shape
        modes = mode_basis.shape[4]
        group = group_size(layers)
        groups = layers // group
        rows_each = round_up(-(-count // group), 8)
        piece_rows = round_up(2 * rows_each + 4, 8)
        size = count // 2 if count % 32 == 0 else count
        chunks = [(first, size) for first in range(0, count, size)]
        anywhere = pl.BlockSpec(memory_space=pltpu.HBM)
        dma = pltpu.SemaphoreType.DMA
        operands = (
            ranks, sources, near_block, expand_basis, compress_basis, mode_basis, down, up,
        )
        return pl.pallas_call(
            functools.partial(kernel, layers, tiles, chunks, rows_each),
            out_shape=pltpu.VMEM(sources.shape, BF16),
            in_specs=[anywhere] * 8,
            out_specs=pl.BlockSpec(memory_space=pltpu.VMEM),
            scratch_shapes=[
                pltpu.SMEM(ranks.shape[1:], jnp.int32),
                pltpu.VMEM(sources.shape[1:], BF16),
                pltpu.VMEM(near_block.shape[2:], BF16),
                pltpu.VMEM(expand_basis.shape[2:], BF16),
                pltpu.VMEM(compress_basis.shape[2:], BF16),
                pltpu.VMEM(mode_basis.shape[2:], BF16),
                pltpu.VMEM((2, 2, modes), F32),
                pltpu.VMEM((max(tiles - 1, 1), 2, count, traces), BF16),
                pltpu.VMEM((2, count, traces), F32),
                pltpu.VMEM((2, count, traces), BF16),
                pltpu.VMEM((2, rows_each * group, modes), F32),
                pltpu.VMEM((group, piece_rows, modes), F32),
                pltpu.VMEM((group, piece_rows, modes), F32),
                pltpu.VMEM((2, piece_rows, modes), F32),
                pltpu.VMEM((groups, piece_rows, modes), F32),
                pltpu.VMEM((group, 2 * rows_each, modes), F32),
                pltpu.VMEM((group, rows_each // 4, 8, modes), BF16),
                pltpu.VMEM((group, rows_each // 4, 8, modes), BF16),
                dma((8,)),
                dma((len(chunks), max(tiles - 1, 1))),
                dma((len(chunks), max(tiles - 1, 1))),
                dma((group,)),
                dma((group,)),
                dma((2, max(groups - 1, 1))),
                dma((groups,)),
                dma((group,)),
                dma((group,)),
            ],
            compiler_params=pltpu.CompilerParams(
                collective_id=0, has_side_effects=True, vmem_limit_bytes=40 * 2**20
            ),
        )(*[pltpu.with_memory_space_constraint(a, pltpu.HBM) for a in operands])

    return jax.shard_map(
        per_device,
        mesh=mesh,
        in_specs=(
            P("layer", None, None, "tile"),
            P("layer", "tile", None, None, None),
            P("layer", "tile", None, None, None, None),
            P("layer", "tile", None, None, None, None),
            P("layer", "tile", None, None, None),
            P("layer", "tile", None, None),
            P("layer", "tile", None, None),
            P("layer", None, None),
        ),
        out_specs=P("layer", None, None, "tile"),
        check_vma=False,
    )
```

```python
import functools

import jax
import jax.numpy as jnp
from jax import lax
from jax.experimental import pallas as pl
from jax.experimental.pallas import tpu as pltpu
from jax.sharding import PartitionSpec as P

MESH = pl.DeviceIdType.MESH
F32 = jnp.float32
BF16 = jnp.bfloat16


def dot(a, b):
    return jnp.dot(a, b, preferred_element_type=F32)


def dot_back(a, b):
    return lax.dot_general(a, b, (((1,), (1,)), ((), ())), preferred_element_type=F32)


def stacked_product(product, stack, b_real, b_imag):
    half = stack.shape[0] // 2
    by_real = product(stack, b_real)
    by_imag = product(stack, b_imag)
    return by_real[:half] - by_imag[half:], by_imag[:half] + by_real[half:]


def times(a, b):
    return a[0] * b[0] - a[1] * b[1], a[0] * b[1] + a[1] * b[0]


def plus(a, b):
    return a[0] + b[0], a[1] + b[1]


def pick(condition, a, b):
    return jnp.where(condition, a[0], b[0]), jnp.where(condition, a[1], b[1])


def chunk_list(count):
    small = count * 3 // 160 * 16
    sizes = [small, small, count - 2 * small] if count % 16 == 0 and small > 0 else [count]
    return [(sum(sizes[:index]), size) for index, size in enumerate(sizes)]


def kernel(
    layers, tiles, chunks,
    ranks_hbm, src_hbm, near_hbm, expand_hbm, compress_hbm, mode_hbm, down_hbm, up_hbm,
    out,
    ranks, src, near, expand, compress, mode, factors, pair_own, pair_in, table,
    others, near_part, fronts, modal, both, folded, arrived, swept, incoming,
    in_sem, src_send, src_recv, factor_send, factor_recv, pair_send, pair_recv,
    half_send, half_recv, far_send, far_recv, back_send, back_recv, known,
):
    layer = lax.axis_index("layer")
    tile = lax.axis_index("tile")
    pairs = layers // 2
    pair = layer // 2
    core = lax.rem(layer, 2)
    partner = (layer + 1 - 2 * core, tile)

    def beyond(at):
        return (at + pairs - pair) // pairs

    def far_device(at):
        return (2 * (at + beyond(at)) + core, tile)

    loads = [
        pltpu.make_async_copy(a, b, in_sem.at[i])
        for i, (a, b) in enumerate(
            [
                (src_hbm.at[0], src),
                (near_hbm.at[0, 0], near),
                (down_hbm.at[0, 0], factors.at[core, 0]),
                (up_hbm.at[0, 0], factors.at[core, 1]),
                (compress_hbm.at[0, 0], compress),
                (expand_hbm.at[0, 0], expand),
                (mode_hbm.at[0, 0], mode),
                (ranks_hbm.at[0], ranks),
            ]
        )
    ]

    barrier = pltpu.get_barrier_semaphore()
    peers = [(layer, lax.rem(tile + tiles - step, tiles)) for step in range(1, tiles)]
    peers += [partner]
    for peer in peers:
        pl.semaphore_signal(barrier, inc=1, device_id=peer, device_id_type=MESH)

    for at in range(pairs):

        @pl.when(at > pair)
        def _(at=at):
            pl.semaphore_signal(
                barrier, inc=1, device_id=(2 * at + core, tile), device_id_type=MESH
            )

    for load in loads:
        load.start()
    pl.semaphore_wait(barrier, len(peers) + pair)

    sources = []
    for index, (first, size) in enumerate(chunks):
        part = []
        for step in range(1, tiles):
            copy = pltpu.make_async_remote_copy(
                src_ref=src_hbm.at[0, :, pl.ds(first, size)],
                dst_ref=others.at[step - 1, :, pl.ds(first, size)],
                send_sem=src_send.at[index, step - 1],
                recv_sem=src_recv.at[index, step - 1],
                device_id=(layer, lax.rem(tile + tiles - step, tiles)),
                device_id_type=MESH,
            )
            copy.start()
            part.append(copy)
        sources.append(part)
    for at in range(pairs):

        @pl.when(at < pair)
        def _(at=at):
            pl.semaphore_signal(known, inc=1, device_id=(2 * at + core, tile), device_id_type=MESH)

    own_factors = [
        pltpu.make_async_remote_copy(
            src_ref=ref.at[0, 0],
            dst_ref=factors.at[core, which],
            send_sem=factor_send.at[which],
            recv_sem=factor_recv.at[which],
            device_id=partner,
            device_id_type=MESH,
        )
        for which, ref in enumerate([down_hbm, up_hbm])
    ]
    for copy in own_factors:
        copy.start()

    loads[0].wait()
    loads[1].wait()
    real, imag = stacked_product(dot, src[...].reshape(-1, src.shape[2]), near[0], near[1])
    near_part[0] = real
    near_part[1] = imag
    for load in loads[2:]:
        load.wait()

    def factor(parity, which):
        return factors[parity, which, 0:1, :], factors[parity, which, 1:2, :]

    for copy in own_factors:
        copy.wait_recv()
    for which in range(2):
        value = times(factor(0, which), factor(1, which))
        pair_own[which, 0:1, :] = value[0]
        pair_own[which, 1:2, :] = value[1]
    def far_copy(source, landing, send, receive, at):
        slot = pair - 1 + beyond(at)
        return pltpu.make_async_remote_copy(
            src_ref=source,
            dst_ref=landing(slot),
            send_sem=send(at),
            recv_sem=receive(slot),
            device_id=far_device(at),
            device_id_type=MESH,
        )

    def far_arrival(source, landing, send, receive, at):
        return pltpu.make_async_remote_copy(
            src_ref=source,
            dst_ref=landing(at),
            send_sem=send(at),
            recv_sem=receive(at),
            device_id=far_device(at),
            device_id_type=MESH,
        )

    pair_refs = (
        pair_own, lambda at: pair_in.at[at], lambda at: pair_send.at[at], lambda at: pair_recv.at[at],
    )
    pair_copies = [
        far_copy(*pair_refs, lax.rem(pair + turn, pairs - 1)) for turn in range(pairs - 1)
    ]

    def make_table():
        for at in range(pairs - 1):
            far_arrival(*pair_refs, at).wait_recv()

        def arrived_factor(at, which):
            return pair_in[at, which, 0:1, :], pair_in[at, which, 1:2, :]

        one = (jnp.ones((1, modal.shape[2]), F32), jnp.zeros((1, modal.shape[2]), F32))
        above, below = {}, {}
        value = one
        for at in range(pairs - 2, -1, -1):
            above[at] = value
            value = pick(at < pair, times(value, arrived_factor(at, 0)), one)
        value = one
        for at in range(pairs - 1):
            below[at] = value
            value = pick(at < pair, one, times(value, arrived_factor(at, 1)))
        for at in range(pairs - 1):
            even = pick(at < pair, above[at], times(factor(1, 1), below[at]))
            odd = pick(at < pair, times(factor(0, 0), above[at]), below[at])
            for row, part in enumerate(even + odd):
                table[at, row : row + 1, :] = part

    half_copies, far_copies, back_copies = {}, {}, {}

    def do_front(index):
        first, size = chunks[index]
        rows = slice(first, first + size)
        real, imag = near_part[0, rows, :], near_part[1, rows, :]
        for step in range(1, tiles):
            sources[index][step - 1].wait_recv()
            source = lax.rem(tile + step, tiles)
            coefficients = stacked_product(
                dot_back,
                others[step - 1, :, rows, :].reshape(2 * size, -1),
                compress[source, 0],
                compress[source, 1],
            )
            stack = jnp.concatenate(coefficients, axis=0)
            kept = lax.broadcasted_iota(jnp.int32, stack.shape, 1) < ranks[tile, source]
            stack = jnp.where(kept, stack, 0.0).astype(BF16)
            far = stacked_product(dot, stack, expand[source, 0], expand[source, 1])
            real, imag = real + far[0], imag + far[1]
        stack = jnp.concatenate([real, imag], axis=0).astype(BF16)
        fronts[:, rows, :] = stack.reshape(2, size, -1)
        real, imag = stacked_product(dot, stack, mode[0], mode[1])
        half = size // 2
        for which in range(2):
            part = slice(which * half, (which + 1) * half)
            modal[which, first : first + half, :] = real[part]
            modal[which, first + half : first + size, :] = imag[part]
        copy = pltpu.make_async_remote_copy(
            src_ref=modal.at[1 - core, pl.ds(first, size)],
            dst_ref=both.at[core, pl.ds(first, size)],
            send_sem=half_send.at[index],
            recv_sem=half_recv.at[index],
            device_id=partner,
            device_id_type=MESH,
        )
        copy.start()
        half_copies[index] = copy
        both[core, rows, :] = modal[core, rows, :]

    def halves(ref, at, index):
        first, size = chunks[index]
        middle = first + size // 2
        return ref[at, first:middle, :], ref[at, middle : first + size, :]

    def far_refs(index):
        first, size = chunks[index]
        return (
            lambda at: arrived.at[at, pl.ds(first, size)],
            lambda at: far_send.at[index, at],
            lambda at: far_recv.at[index, at],
        )

    def do_fold(index):
        first, size = chunks[index]
        half_copies[index].wait_recv()
        even, odd = halves(both, 0, index), halves(both, 1, index)
        down = plus(times(factor(1, 0), even), odd)
        up = plus(even, times(factor(0, 1), odd))
        for which, value in enumerate([down, up]):
            folded[which, first : first + size, :] = jnp.concatenate(value, axis=0).astype(BF16)
        copies = [
            far_copy(folded.at[1 - beyond(at), pl.ds(first, size)], *far_refs(index), at)
            for at in [lax.rem(pair + turn, pairs - 1) for turn in range(pairs - 1)]
        ]
        for copy in copies:
            copy.start()
        far_copies[index] = copies

    def do_sweep(index):
        first, size = chunks[index]
        half = size // 2
        for at in range(pairs - 1):
            far_arrival(folded.at[0, pl.ds(first, size)], *far_refs(index), at).wait_recv()
        even, odd = halves(both, 1, index), halves(both, 0, index)
        for slot in range(pairs - 1):
            value = arrived[slot, first : first + size, :].astype(F32)
            value = value[:half], value[half:]
            row = [table[slot, at : at + 1, :] for at in range(4)]
            even = plus(even, times(row[0:2], value))
            odd = plus(odd, times(row[2:4], value))
        for which, value in enumerate([even, odd]):
            swept[which, first : first + size, :] = jnp.concatenate(value, axis=0).astype(BF16)
        copy = pltpu.make_async_remote_copy(
            src_ref=swept.at[1 - core, pl.ds(first, size)],
            dst_ref=incoming.at[core, pl.ds(first, size)],
            send_sem=back_send.at[index],
            recv_sem=back_recv.at[index],
            device_id=partner,
            device_id_type=MESH,
        )
        copy.start()
        back_copies[index] = copy
        incoming[core, first : first + size, :] = swept[core, first : first + size, :]

    def do_back(index):
        first, size = chunks[index]
        half = size // 2
        rows = slice(first, first + size)
        back_copies[index].wait_recv()
        stack = incoming[:, rows, :].reshape(2 * size, -1)
        by_real, by_imag = dot_back(stack, mode[0]), dot_back(stack, mode[1])
        reals, imags = [], []
        for which in range(2):
            real = slice(which * size, which * size + half)
            imag = slice(which * size + half, (which + 1) * size)
            reals.append(by_real[real] - by_imag[imag])
            imags.append(by_imag[real] + by_real[imag])
        stack = jnp.concatenate(reals + imags, axis=0).astype(BF16)
        real, imag = stacked_product(dot, stack, near[0], near[1])
        out[0, 0, rows, :] = (fronts[0, rows, :].astype(F32) + real).astype(BF16)
        out[0, 1, rows, :] = (fronts[1, rows, :].astype(F32) + imag).astype(BF16)

    for index in range(len(chunks)):
        do_front(index)
        if index == 0:

            @pl.when(pair < pairs - 1)
            def _():
                pl.semaphore_wait(known, pairs - 1 - pair)

            for copy in pair_copies:
                copy.start()
        do_fold(index)
    make_table()
    for index in range(len(chunks)):
        do_sweep(index)
        do_back(index)

    everything = [copy for part in sources for copy in part] + own_factors + pair_copies
    everything += [copy for copies in far_copies.values() for copy in copies]
    everything += list(half_copies.values()) + list(back_copies.values())
    for copy in everything:
        copy.wait_send()


def solution(mesh):
    layers = mesh.shape["layer"]
    tiles = mesh.shape["tile"]

    def per_device(sources, near_block, expand_basis, compress_basis, mode_basis, down, up, ranks):
        _, _, count, traces = sources.shape
        modes = mode_basis.shape[4]
        pairs = layers // 2
        far = max(pairs - 1, 1)
        near_tiles = max(tiles - 1, 1)
        chunks = chunk_list(count)
        total = len(chunks)
        anywhere = pl.BlockSpec(memory_space=pltpu.HBM)
        dma = pltpu.SemaphoreType.DMA
        operands = (
            ranks, sources, near_block, expand_basis, compress_basis, mode_basis, down, up,
        )
        return pl.pallas_call(
            functools.partial(kernel, layers, tiles, chunks),
            out_shape=pltpu.VMEM(sources.shape, BF16),
            in_specs=[anywhere] * 8,
            out_specs=pl.BlockSpec(memory_space=pltpu.VMEM),
            scratch_shapes=[
                pltpu.SMEM(ranks.shape[1:], jnp.int32),
                pltpu.VMEM(sources.shape[1:], BF16),
                pltpu.VMEM(near_block.shape[2:], BF16),
                pltpu.VMEM(expand_basis.shape[2:], BF16),
                pltpu.VMEM(compress_basis.shape[2:], BF16),
                pltpu.VMEM(mode_basis.shape[2:], BF16),
                pltpu.VMEM((2, 2, 2, modes), F32),
                pltpu.VMEM((2, 2, modes), F32),
                pltpu.VMEM((far, 2, 2, modes), F32),
                pltpu.VMEM((far, 4, modes), F32),
                pltpu.VMEM((near_tiles, 2, count, traces), BF16),
                pltpu.VMEM((2, count, traces), F32),
                pltpu.VMEM((2, count, traces), BF16),
                pltpu.VMEM((2, count, modes), F32),
                pltpu.VMEM((2, count, modes), F32),
                pltpu.VMEM((2, count, modes), BF16),
                pltpu.VMEM((far, count, modes), BF16),
                pltpu.VMEM((2, count, modes), BF16),
                pltpu.VMEM((2, count, modes), BF16),
                dma((8,)),
                dma((total, near_tiles)),
                dma((total, near_tiles)),
                dma((2,)),
                dma((2,)),
                dma((far,)),
                dma((far,)),
                dma((total,)),
                dma((total,)),
                dma((total, far)),
                dma((total, far)),
                dma((total,)),
                dma((total,)),
                pltpu.SemaphoreType.REGULAR,
            ],
            compiler_params=pltpu.CompilerParams(
                collective_id=0, has_side_effects=True, vmem_limit_bytes=40 * 2**20
            ),
        )(*[pltpu.with_memory_space_constraint(a, pltpu.HBM) for a in operands])

    return jax.shard_map(
        per_device,
        mesh=mesh,
        in_specs=(
            P("layer", None, None, "tile"),
            P("layer", "tile", None, None, None),
            P("layer", "tile", None, None, None, None),
            P("layer", "tile", None, None, None, None),
            P("layer", "tile", None, None, None),
            P("layer", "tile", None, None),
            P("layer", "tile", None, None),
            P("layer", None, None),
        ),
        out_specs=P("layer", None, None, "tile"),
        check_vma=False,
    )
```

```python
import functools

import jax
import jax.numpy as jnp
from jax import lax
from jax.experimental import pallas as pl
from jax.experimental.pallas import tpu as pltpu
from jax.sharding import PartitionSpec as P

MESH = pl.DeviceIdType.MESH
F32 = jnp.float32
BF16 = jnp.bfloat16


def dot(a, b):
    return jnp.dot(a, b, preferred_element_type=F32)


def dot_back(a, b):
    return lax.dot_general(a, b, (((1,), (1,)), ((), ())), preferred_element_type=F32)


def stacked_product(product, stack, b_real, b_imag):
    half = stack.shape[0] // 2
    by_real = product(stack, b_real)
    by_imag = product(stack, b_imag)
    return by_real[:half] - by_imag[half:], by_imag[:half] + by_real[half:]


def times(a, b):
    return a[0] * b[0] - a[1] * b[1], a[0] * b[1] + a[1] * b[0]


def plus(a, b):
    return a[0] + b[0], a[1] + b[1]


def pick(condition, a, b):
    return jnp.where(condition, a[0], b[0]), jnp.where(condition, a[1], b[1])


def chunk_list(count):
    small = count * 3 // 160 * 16
    sizes = [small, small, count - 2 * small] if count % 16 == 0 and small > 0 else [count]
    return [(sum(sizes[:index]), size) for index, size in enumerate(sizes)]


def kernel(
    layers, tiles, chunks,
    ranks_hbm, src_hbm, near_hbm, expand_hbm, compress_hbm, mode_hbm, down_hbm, up_hbm,
    out,
    ranks, src, near, expand, compress, mode, factors, pair_own, pair_in, table,
    others, near_part, near_modal, expand_modal, fronts, modal, both, folded, arrived, swept, incoming,
    in_sem, src_send, src_recv, factor_send, factor_recv, pair_send, pair_recv,
    half_send, half_recv, far_send, far_recv, back_send, back_recv, known,
):
    layer = lax.axis_index("layer")
    tile = lax.axis_index("tile")
    pairs = layers // 2
    pair = layer // 2
    core = lax.rem(layer, 2)
    partner = (layer + 1 - 2 * core, tile)

    def beyond(at):
        return (at + pairs - pair) // pairs

    def far_device(at):
        return (2 * (at + beyond(at)) + core, tile)

    loads = [
        pltpu.make_async_copy(a, b, in_sem.at[i])
        for i, (a, b) in enumerate(
            [
                (src_hbm.at[0], src),
                (near_hbm.at[0, 0], near),
                (down_hbm.at[0, 0], factors.at[core, 0]),
                (up_hbm.at[0, 0], factors.at[core, 1]),
                (compress_hbm.at[0, 0], compress),
                (expand_hbm.at[0, 0], expand),
                (mode_hbm.at[0, 0], mode),
                (ranks_hbm.at[0], ranks),
            ]
        )
    ]

    barrier = pltpu.get_barrier_semaphore()
    peers = [(layer, lax.rem(tile + tiles - step, tiles)) for step in range(1, tiles)]
    peers += [partner]
    for peer in peers:
        pl.semaphore_signal(barrier, inc=1, device_id=peer, device_id_type=MESH)

    for at in range(pairs):

        @pl.when(at > pair)
        def _(at=at):
            pl.semaphore_signal(
                barrier, inc=1, device_id=(2 * at + core, tile), device_id_type=MESH
            )

    for load in loads:
        load.start()
    pl.semaphore_wait(barrier, len(peers) + pair)

    sources = []
    for index, (first, size) in enumerate(chunks):
        part = []
        for step in range(1, tiles):
            copy = pltpu.make_async_remote_copy(
                src_ref=src_hbm.at[0, :, pl.ds(first, size)],
                dst_ref=others.at[step - 1, :, pl.ds(first, size)],
                send_sem=src_send.at[index, step - 1],
                recv_sem=src_recv.at[index, step - 1],
                device_id=(layer, lax.rem(tile + tiles - step, tiles)),
                device_id_type=MESH,
            )
            part.append(copy)
        sources.append(part)

    def send_sources(index):
        if index < len(chunks):
            for copy in sources[index]:
                copy.start()

    send_sources(0)
    for at in range(pairs):

        @pl.when(at < pair)
        def _(at=at):
            pl.semaphore_signal(known, inc=1, device_id=(2 * at + core, tile), device_id_type=MESH)

    own_factors = [
        pltpu.make_async_remote_copy(
            src_ref=ref.at[0, 0],
            dst_ref=factors.at[core, which],
            send_sem=factor_send.at[which],
            recv_sem=factor_recv.at[which],
            device_id=partner,
            device_id_type=MESH,
        )
        for which, ref in enumerate([down_hbm, up_hbm])
    ]
    for copy in own_factors:
        copy.start()

    loads[0].wait()
    loads[1].wait()
    real, imag = stacked_product(dot, src[...].reshape(-1, src.shape[2]), near[0], near[1])
    near_part[0] = real
    near_part[1] = imag
    for load in loads[2:]:
        load.wait()
    stack = near_part[...].reshape(-1, near_part.shape[2]).astype(BF16)
    real, imag = stacked_product(dot, stack, mode[0], mode[1])
    near_modal[0] = real
    near_modal[1] = imag
    for step in range(1, tiles):
        source = lax.rem(tile + step, tiles)
        stack = expand[source].reshape(-1, expand.shape[3])
        real, imag = stacked_product(dot, stack, mode[0], mode[1])
        expand_modal[step - 1, 0] = real.astype(BF16)
        expand_modal[step - 1, 1] = imag.astype(BF16)

    def factor(parity, which):
        return factors[parity, which, 0:1, :], factors[parity, which, 1:2, :]

    for copy in own_factors:
        copy.wait_recv()
    for which in range(2):
        value = times(factor(0, which), factor(1, which))
        pair_own[which, 0:1, :] = value[0]
        pair_own[which, 1:2, :] = value[1]
    def far_copy(source, landing, send, receive, at):
        slot = pair - 1 + beyond(at)
        return pltpu.make_async_remote_copy(
            src_ref=source,
            dst_ref=landing(slot),
            send_sem=send(at),
            recv_sem=receive(slot),
            device_id=far_device(at),
            device_id_type=MESH,
        )

    def far_arrival(source, landing, send, receive, at):
        return pltpu.make_async_remote_copy(
            src_ref=source,
            dst_ref=landing(at),
            send_sem=send(at),
            recv_sem=receive(at),
            device_id=far_device(at),
            device_id_type=MESH,
        )

    send_sources(1)

    pair_refs = (
        pair_own, lambda at: pair_in.at[at], lambda at: pair_send.at[at], lambda at: pair_recv.at[at],
    )
    pair_copies = [
        far_copy(*pair_refs, lax.rem(pair + turn, pairs - 1)) for turn in range(pairs - 1)
    ]

    def make_table():
        for at in range(pairs - 1):
            far_arrival(*pair_refs, at).wait_recv()

        def arrived_factor(at, which):
            return pair_in[at, which, 0:1, :], pair_in[at, which, 1:2, :]

        one = (jnp.ones((1, modal.shape[2]), F32), jnp.zeros((1, modal.shape[2]), F32))
        above, below = {}, {}
        value = one
        for at in range(pairs - 2, -1, -1):
            above[at] = value
            value = pick(at < pair, times(value, arrived_factor(at, 0)), one)
        value = one
        for at in range(pairs - 1):
            below[at] = value
            value = pick(at < pair, one, times(value, arrived_factor(at, 1)))
        for at in range(pairs - 1):
            even = pick(at < pair, above[at], times(factor(1, 1), below[at]))
            odd = pick(at < pair, times(factor(0, 0), above[at]), below[at])
            for row, part in enumerate(even + odd):
                table[at, row : row + 1, :] = part

    half_copies, far_copies, back_copies = {}, {}, {}

    def do_front(index):
        first, size = chunks[index]
        rows = slice(first, first + size)
        real, imag = near_modal[0, rows, :], near_modal[1, rows, :]
        stacks = []
        for step in range(1, tiles):
            sources[index][step - 1].wait_recv()
            if step == tiles - 1:
                send_sources(index + 2)
            source = lax.rem(tile + step, tiles)
            coefficients = stacked_product(
                dot_back,
                others[step - 1, :, rows, :].reshape(2 * size, -1),
                compress[source, 0],
                compress[source, 1],
            )
            stack = jnp.concatenate(coefficients, axis=0)
            kept = lax.broadcasted_iota(jnp.int32, stack.shape, 1) < ranks[tile, source]
            stack = jnp.where(kept, stack, 0.0).astype(BF16)
            far = stacked_product(dot, stack, expand_modal[step - 1, 0], expand_modal[step - 1, 1])
            real, imag = real + far[0], imag + far[1]
            stacks.append(stack)
        half = size // 2
        for which in range(2):
            part = slice(which * half, (which + 1) * half)
            modal[which, first : first + half, :] = real[part]
            modal[which, first + half : first + size, :] = imag[part]
        copy = pltpu.make_async_remote_copy(
            src_ref=modal.at[1 - core, pl.ds(first, size)],
            dst_ref=both.at[core, pl.ds(first, size)],
            send_sem=half_send.at[index],
            recv_sem=half_recv.at[index],
            device_id=partner,
            device_id_type=MESH,
        )
        copy.start()
        half_copies[index] = copy
        both[core, rows, :] = modal[core, rows, :]
        real, imag = near_part[0, rows, :], near_part[1, rows, :]
        for step, stack in enumerate(stacks, 1):
            source = lax.rem(tile + step, tiles)
            far = stacked_product(dot, stack, expand[source, 0], expand[source, 1])
            real, imag = real + far[0], imag + far[1]
        fronts[0, rows, :] = real.astype(BF16)
        fronts[1, rows, :] = imag.astype(BF16)

    def halves(ref, at, index):
        first, size = chunks[index]
        middle = first + size // 2
        return ref[at, first:middle, :], ref[at, middle : first + size, :]

    def far_refs(index):
        first, size = chunks[index]
        return (
            lambda at: arrived.at[at, pl.ds(first, size)],
            lambda at: far_send.at[index, at],
            lambda at: far_recv.at[index, at],
        )

    def do_fold(index):
        first, size = chunks[index]
        half_copies[index].wait_recv()
        even, odd = halves(both, 0, index), halves(both, 1, index)
        down = plus(times(factor(1, 0), even), odd)
        up = plus(even, times(factor(0, 1), odd))
        for which, value in enumerate([down, up]):
            folded[which, first : first + size, :] = jnp.concatenate(value, axis=0).astype(BF16)
        copies = [
            far_copy(folded.at[1 - beyond(at), pl.ds(first, size)], *far_refs(index), at)
            for at in [lax.rem(pair + turn, pairs - 1) for turn in range(pairs - 1)]
        ]
        for copy in copies:
            copy.start()
        far_copies[index] = copies

    def do_sweep(index):
        first, size = chunks[index]
        half = size // 2
        even, odd = halves(both, 1, index), halves(both, 0, index)
        for slot in range(pairs - 1):
            far_arrival(folded.at[0, pl.ds(first, size)], *far_refs(index), slot).wait_recv()
            value = arrived[slot, first : first + size, :].astype(F32)
            value = value[:half], value[half:]
            row = [table[slot, at : at + 1, :] for at in range(4)]
            even = plus(even, times(row[0:2], value))
            odd = plus(odd, times(row[2:4], value))
        for which, value in enumerate([even, odd]):
            swept[which, first : first + size, :] = jnp.concatenate(value, axis=0).astype(BF16)
        copy = pltpu.make_async_remote_copy(
            src_ref=swept.at[1 - core, pl.ds(first, size)],
            dst_ref=incoming.at[core, pl.ds(first, size)],
            send_sem=back_send.at[index],
            recv_sem=back_recv.at[index],
            device_id=partner,
            device_id_type=MESH,
        )
        copy.start()
        back_copies[index] = copy
        incoming[core, first : first + size, :] = swept[core, first : first + size, :]

    def do_back(index):
        first, size = chunks[index]
        half = size // 2
        rows = slice(first, first + size)
        back_copies[index].wait_recv()
        stack = incoming[:, rows, :].reshape(2 * size, -1)
        by_real, by_imag = dot_back(stack, mode[0]), dot_back(stack, mode[1])
        reals, imags = [], []
        for which in range(2):
            real = slice(which * size, which * size + half)
            imag = slice(which * size + half, (which + 1) * size)
            reals.append(by_real[real] - by_imag[imag])
            imags.append(by_imag[real] + by_real[imag])
        stack = jnp.concatenate(reals + imags, axis=0).astype(BF16)
        real, imag = stacked_product(dot, stack, near[0], near[1])
        out[0, 0, rows, :] = (fronts[0, rows, :].astype(F32) + real).astype(BF16)
        out[0, 1, rows, :] = (fronts[1, rows, :].astype(F32) + imag).astype(BF16)

    for index in range(len(chunks)):
        do_front(index)
        if index == 0:

            @pl.when(pair < pairs - 1)
            def _():
                pl.semaphore_wait(known, pairs - 1 - pair)

        do_fold(index)
        if index == 0:
            for copy in pair_copies:
                copy.start()
    make_table()
    for index in range(len(chunks)):
        if index == len(chunks) - 1:
            sent = [copy for part in sources for copy in part] + own_factors + pair_copies
            sent += [copy for copies in far_copies.values() for copy in copies]
            sent += list(half_copies.values()) + list(back_copies.values())
            for copy in sent:
                copy.wait_send()
        do_sweep(index)
        do_back(index)
    back_copies[len(chunks) - 1].wait_send()


def solution(mesh):
    layers = mesh.shape["layer"]
    tiles = mesh.shape["tile"]

    def per_device(sources, near_block, expand_basis, compress_basis, mode_basis, down, up, ranks):
        _, _, count, traces = sources.shape
        modes = mode_basis.shape[4]
        pairs = layers // 2
        far = max(pairs - 1, 1)
        near_tiles = max(tiles - 1, 1)
        chunks = chunk_list(count)
        total = len(chunks)
        anywhere = pl.BlockSpec(memory_space=pltpu.HBM)
        dma = pltpu.SemaphoreType.DMA
        operands = (
            ranks, sources, near_block, expand_basis, compress_basis, mode_basis, down, up,
        )
        return pl.pallas_call(
            functools.partial(kernel, layers, tiles, chunks),
            out_shape=pltpu.VMEM(sources.shape, BF16),
            in_specs=[anywhere] * 8,
            out_specs=pl.BlockSpec(memory_space=pltpu.VMEM),
            scratch_shapes=[
                pltpu.SMEM(ranks.shape[1:], jnp.int32),
                pltpu.VMEM(sources.shape[1:], BF16),
                pltpu.VMEM(near_block.shape[2:], BF16),
                pltpu.VMEM(expand_basis.shape[2:], BF16),
                pltpu.VMEM(compress_basis.shape[2:], BF16),
                pltpu.VMEM(mode_basis.shape[2:], BF16),
                pltpu.VMEM((2, 2, 2, modes), F32),
                pltpu.VMEM((2, 2, modes), F32),
                pltpu.VMEM((far, 2, 2, modes), F32),
                pltpu.VMEM((far, 4, modes), F32),
                pltpu.VMEM((near_tiles, 2, count, traces), BF16),
                pltpu.VMEM((2, count, traces), F32),
                pltpu.VMEM((2, count, modes), F32),
                pltpu.VMEM((near_tiles, 2, expand_basis.shape[4], modes), BF16),
                pltpu.VMEM((2, count, traces), BF16),
                pltpu.VMEM((2, count, modes), F32),
                pltpu.VMEM((2, count, modes), F32),
                pltpu.VMEM((2, count, modes), BF16),
                pltpu.VMEM((far, count, modes), BF16),
                pltpu.VMEM((2, count, modes), BF16),
                pltpu.VMEM((2, count, modes), BF16),
                dma((8,)),
                dma((total, near_tiles)),
                dma((total, near_tiles)),
                dma((2,)),
                dma((2,)),
                dma((far,)),
                dma((far,)),
                dma((total,)),
                dma((total,)),
                dma((total, far)),
                dma((total, far)),
                dma((total,)),
                dma((total,)),
                pltpu.SemaphoreType.REGULAR,
            ],
            compiler_params=pltpu.CompilerParams(
                collective_id=0, has_side_effects=True, vmem_limit_bytes=40 * 2**20
            ),
        )(*[pltpu.with_memory_space_constraint(a, pltpu.HBM) for a in operands])

    return jax.shard_map(
        per_device,
        mesh=mesh,
        in_specs=(
            P("layer", None, None, "tile"),
            P("layer", "tile", None, None, None),
            P("layer", "tile", None, None, None, None),
            P("layer", "tile", None, None, None, None),
            P("layer", "tile", None, None, None),
            P("layer", "tile", None, None),
            P("layer", "tile", None, None),
            P("layer", None, None),
        ),
        out_specs=P("layer", None, None, "tile"),
        check_vma=False,
    )
```
